256 devices in a mesh: normal: 64 (over x, z, core), span: 4 (over y).
Axes of the slice: x: 4, y: 4, z: 8, core: 2. Of those that a mesh axis runs over, the one named last changes fastest.
Arguments:
- density: float32 [1024, 32, 128], P('normal', 'span'), may hold values from 0.5 to 2
- velocity: float32 [1024, 3, 32, 128], P('normal', None, 'span'), may hold values from -4 to 4
- pressure: float32 [1024, 32, 128], P('normal', 'span'), may hold values from 0.5 to 2
- face_coef: float32 [1024, 5, 5, 32, 128], P('normal', None, None, 'span'), as said below
Outputs:
- update: float32 [1024, 5, 32, 128], P('normal', None, 'span')
The draws below stay inside these ranges and needn't reach their ends.
Inputs may be any that keep to these rules, and one draw needn't show every extreme that they name: Every 5x5 block face_coef[j, :, :, k, i] is symmetric positive definite with smallest eigenvalue at least 0.1.
All inputs are finite; a program needn't handle non-finite values.
Results may differ from the reference program's by a relative error of at most 0.0003.
Values sent between devices are 32-bit elements; how exact they have to be, the bound alone decides.
A program may use at most 192 MiB of HBM per device.

```python
import jax
import jax.numpy as jnp
from jax import lax

NI = 128
DIFFUSION = 1000
NJ = 1024
NK = 32


def draw_face_coef(key, part):
    key_mix = jax.random.fold_in(key, 11)
    key_floor = jax.random.fold_in(key, 12)
    mixing = jnp.clip(jax.random.normal(key_mix, (NJ, 5, 5, NK, NI), jnp.float32), -3.0, 3.0)
    coupled = jnp.einsum('jabki,jcbki->jacki', mixing, mixing) / 5.0
    floor_term = jnp.exp(jax.random.uniform(key_floor, (NJ, 1, 1, NK, NI), jnp.float32, jnp.log(0.5), jnp.log(2.0)))
    identity = jnp.eye(5, dtype=jnp.float32)[None, :, :, None, None]
    blocks = coupled + floor_term * identity
    return blocks


def levels(rng, shape, shards, smallest, largest):
    loudness, own = 1.0, jax.random.fold_in(rng, 6)
    for dim, parts in shards:
        heights = jnp.exp(jax.random.uniform(jax.random.fold_in(own, dim), (parts,), jnp.float32, smallest / len(shards), largest / len(shards)))
        loudness = loudness * jnp.repeat(heights, shape[dim] // parts).reshape([-1 if axis == dim else 1 for axis in range(len(shape))])
    return loudness


def normal_values(own_key, dims, width, most, cuts=(), held_as=jnp.bfloat16):
    factor_of = levels(own_key, dims, cuts, -0.22, 0.18) if cuts else 1.0
    array = jax.random.normal(own_key, dims, jnp.float32) * width * factor_of
    return jnp.minimum(jnp.maximum(array, -most), most).astype(held_as)


def setup_inputs(seed: int = 0) -> dict:
    streams_of = jax.random.split(jax.random.key(seed), 5)
    density = jnp.clip(0.5 + 1.5 * jax.random.uniform(streams_of[0], (NJ, NK, NI), jnp.float32) ** levels(streams_of[0], (NJ, NK, NI), ((0, 64), (1, 4)), -0.2, 0.2), 0.5, 2.0)
    velocity = normal_values(streams_of[1], (NJ, 3, NK, NI), 1.0, 4.0, ((0, 64), (2, 4)), jnp.float32)
    pressure = jnp.clip(0.5 + 1.5 * jax.random.uniform(streams_of[2], (NJ, NK, NI), jnp.float32) ** levels(streams_of[2], (NJ, NK, NI), ((0, 64), (1, 4)), -0.2, 0.2), 0.5, 2.0)
    face_coef = draw_face_coef(jax.random.fold_in(streams_of[4], 71), 0)
    return {"density": density, "velocity": velocity, "pressure": pressure, "face_coef": face_coef}


gamma_gas = 1.4
time_step = 50.0


def fluxes(density, velocity, pressure):
    speed_sq = jnp.sum(velocity * velocity, axis=1)
    energy = pressure / (gamma_gas - 1.0) + 0.5 * density * speed_sq
    momentum = density[:, None] * velocity
    result = []
    for direction in range(3):
        along_vel = velocity[:, direction]
        pieces = [density * along_vel]
        for component in range(3):
            moment_flux = momentum[:, component] * along_vel
            if component == direction:
                moment_flux = moment_flux + pressure
            pieces.append(moment_flux)
        pieces.append((energy + pressure) * along_vel)
        result.append(jnp.stack(pieces, axis=1))
    return result


def stencil(plus_one, minus_one, plus_two, minus_two):
    return (8.0 * (plus_one - minus_one) - (plus_two - minus_two)) / 12.0


def along_zero(field, dim_index):
    length = field.shape[dim_index]
    widths = [(0, 0)] * field.ndim
    widths[dim_index] = (2, 2)
    padded = jnp.pad(field, widths)

    def shifted(begin):
        return lax.slice_in_dim(padded, begin, begin + length, axis=dim_index)

    return stencil(shifted(3), shifted(1), shifted(4), shifted(0))


def along_wrap(field, dim_index):
    return stencil(jnp.roll(field, -1, dim_index), jnp.roll(field, 1, dim_index),
                   jnp.roll(field, -2, dim_index), jnp.roll(field, 2, dim_index))


def product(left_block, right_block):
    return jnp.sum(left_block[:, :, None, :] * right_block[None, :, :, :], axis=1)


def eliminate(matrix, values):
    count = matrix.shape[0]
    matrix_rows = [matrix[i] for i in range(count)]
    value_rows = [values[i] for i in range(count)]
    for pivot_at in range(count):
        inverse = 1.0 / matrix_rows[pivot_at][pivot_at]
        matrix_rows[pivot_at] = matrix_rows[pivot_at] * inverse
        value_rows[pivot_at] = value_rows[pivot_at] * inverse
        for other in range(count):
            if other != pivot_at:
                factor = matrix_rows[other][pivot_at]
                matrix_rows[other] = matrix_rows[other] - factor * matrix_rows[pivot_at]
                value_rows[other] = value_rows[other] - factor * value_rows[pivot_at]
    return jnp.stack(value_rows)


def line_solve(upper_faces, lower_faces, sources):
    line_count = upper_faces.shape[-1]
    columns_count = sources.shape[2]
    unit_block = jnp.eye(5, dtype=jnp.float32)[:, :, None]
    coeff = jnp.float32(DIFFUSION)

    def forward(state_pair, row_data):
        coupled_prev, partial_prev = state_pair
        upper_face, lower_face, values = row_data
        lower = -coeff * lower_face
        matrix = unit_block + coeff * (lower_face + upper_face) - product(lower, coupled_prev)
        columns = jnp.concatenate([-coeff * upper_face, values - product(lower, partial_prev)], axis=1)
        solved = eliminate(matrix, columns)
        updated = (solved[:, :5], solved[:, 5:])
        return updated, updated

    initial = (jnp.zeros((5, 5, line_count), jnp.float32), jnp.zeros((5, columns_count, line_count), jnp.float32))
    _, (coupled, partial_value) = lax.scan(forward, initial, (upper_faces, lower_faces, sources))

    def backward(next_value, row_data):
        coupled_row, partial_row = row_data
        value = partial_row - product(coupled_row, next_value)
        return value, value

    _, solved = lax.scan(backward, jnp.zeros((5, columns_count, line_count), jnp.float32), (coupled, partial_value), reverse=True)
    return solved


def reference(density, velocity, pressure, face_coef):
    rows_normal, _, cells_span, cells_stream = velocity.shape
    flux_stream, flux_normal, flux_span = fluxes(density, velocity, pressure)
    residual = -(along_zero(flux_stream, 3) + along_zero(flux_normal, 0) + along_wrap(flux_span, 2))
    source = time_step * residual
    line_count = cells_span * cells_stream
    upper_faces = face_coef.reshape(rows_normal, 5, 5, line_count)
    lower_faces = jnp.concatenate([jnp.zeros_like(upper_faces[:1]), upper_faces[:-1]], axis=0)
    solved = line_solve(upper_faces, lower_faces, source.reshape(rows_normal, 5, 1, line_count))
    return solved.reshape(rows_normal, 5, cells_span, cells_stream)
```

```python
import jax
import jax.numpy as jnp
from jax import lax
from jax.experimental import pallas as pl
from jax.experimental.pallas import tpu as pltpu
from jax.sharding import PartitionSpec as P

MESH = pl.DeviceIdType.MESH
DIFFUSION = 1000.0
GAMMA = 1.4
STEP = 50.0
NX, NZ, NC, NS = 4, 8, 2, 4
CELLS = 16
FIVE = range(5)
LL, RR, LR, RL, RH, ELEM = 0, 15, 30, 55, 60, 65
KEPT = 55
ZROWS, BROWS = 72, 16
ORDER = (4, 3, 5, 2, 6, 1, 7)


def tri(i, j):
    low, high = min(i, j), max(i, j)
    return low * 5 - low * (low - 1) // 2 + high - low


def total(terms):
    terms = list(terms)
    while len(terms) > 1:
        terms = [a + b for a, b in zip(terms[::2], terms[1::2])] + terms[len(terms) & ~1 :]
    return terms[0]


def sym_inverse(upper):
    a = list(upper)
    for p in FIVE:
        d = 1.0 / a[tri(p, p)]
        row = [a[tri(p, j)] for j in FIVE]
        scaled = [row[j] * d for j in FIVE]
        for i in FIVE:
            for j in range(i, 5):
                if p not in (i, j):
                    a[tri(i, j)] = a[tri(i, j)] - scaled[i] * row[j]
        for j in FIVE:
            if j != p:
                a[tri(p, j)] = scaled[j]
        a[tri(p, p)] = -d
    return [-v for v in a]


def inverse(rows):
    a = [list(row) for row in rows]
    for p in FIVE:
        d = 1.0 / a[p][p]
        top = [d if j == p else a[p][j] * d for j in FIVE]
        for i in FIVE:
            if i != p:
                f = a[i][p]
                a[i] = [-f * d if j == p else a[i][j] - f * top[j] for j in FIVE]
        a[p] = top
    return a


def combine(left, right, put, keep):
    middle = left(RR, 15) + right(LL, 15)
    inv = sym_inverse([middle[t] for t in range(15)])
    lr1 = [left(LR + 5 * i, 5) for i in FIVE]
    lr2 = [right(LR + 5 * i, 5) for i in FIVE]
    lt1 = [jnp.stack([lr1[i][k] for i in FIVE]) for k in FIVE]
    load = left(RH, 5) + right(RL, 5)
    w1 = [total(inv[tri(i, k)][None] * lt1[k] for k in FIVE) for i in FIVE]
    w2 = [total(inv[tri(i, k)][None] * lr2[k] for k in FIVE) for i in FIVE]
    w = [total(inv[tri(i, k)] * load[k] for k in FIVE) for i in FIVE]
    for i in FIVE:
        keep(5 * i, w1[i])
        keep(25 + 5 * i, w2[i])
        keep(50 + i, w[i][None])
    for i in FIVE:
        t = tri(i, i)
        put(LL + t, left(LL + t, 5 - i) - total(lr1[i][k][None] * w1[k][i:] for k in FIVE))
        put(RR + t, right(RR + t, 5 - i) - total(lr2[k][i][None] * w2[k][i:] for k in FIVE))
        put(LR + 5 * i, -total(lr1[i][k][None] * w2[k] for k in FIVE))
        put(RL + i, left(RL + i, 1) - total(lr1[i][k] * w[k] for k in FIVE)[None])
        put(RH + i, right(RH + i, 1) - total(lr2[k][i] * w[k] for k in FIVE)[None])


def middle_value(kept, low, high):
    rows = []
    for i in FIVE:
        near, far = kept(5 * i, 5), kept(25 + 5 * i, 5)
        rows.append(kept(50 + i, 1)[0] - total(total((near * low, far * high))[k] for k in FIVE))
    return jnp.stack(rows)


def flux(d, v, p, direction):
    along = v[direction]
    energy = p / (GAMMA - 1.0) + 0.5 * d * (v[0] * v[0] + v[1] * v[1] + v[2] * v[2])
    carried = d * along
    pieces = [carried]
    for component in range(3):
        piece = carried * v[component]
        pieces.append(piece + p if component == direction else piece)
    pieces.append((energy + p) * along)
    return pieces


def kernel(
    den, vel, pre, fac, out,
    kf, pd, pv, pp, comp, src, fn, ld, lv, lp, hd, hv, hp, spk, srv, gs, ee, wp, pe,
    zs, zr, ze, wz, xs, xr, xe, wx, bs, br,
    load_sem, near_send, near_recv, z_send, z_recv, x_send, x_recv, b_send, b_recv,
):
    me, row = lax.axis_index("normal"), lax.axis_index("span")
    core = lax.rem(me, NC)
    z = lax.rem(lax.div(me, NC), NZ)
    x = lax.div(me, NC * NZ)
    count = NX * NZ * NC

    def place(x_at, z_at, core_at):
        return ((x_at * NZ + z_at) * NC + core_at, row)

    above = (lax.rem(me + 1, count), row)
    below = (lax.rem(me + count - 1, count), row)
    ahead = (me, lax.rem(row + 1, NS))
    behind = (me, lax.rem(row + NS - 1, NS))
    partner = place(x, z, 1 - core)

    barrier = pltpu.get_barrier_semaphore()
    met = [above, below, ahead, behind, partner]
    met += [place(x, lax.rem(z + o, NZ), c) for o in range(1, NZ) for c in range(NC)]
    met += [place(lax.rem(x + o, NX), z, core) for o in range(1, NX)]
    loads = [
        pltpu.make_async_copy(fac, kf, load_sem.at[0]),
        pltpu.make_async_copy(den, pd, load_sem.at[1]),
        pltpu.make_async_copy(vel, pv, load_sem.at[2]),
        pltpu.make_async_copy(pre, pp, load_sem.at[3]),
    ]
    for copy in loads[1:] + loads[:1]:
        copy.start()
    for device in met:
        pl.semaphore_signal(barrier, inc=1, device_id=device, device_id_type=MESH)
    for copy in loads[1:]:
        copy.wait()

    def send(source, target, number, device):
        return pltpu.make_async_remote_copy(
            src_ref=source, dst_ref=target, send_sem=near_send.at[number],
            recv_sem=near_recv.at[number], device_id=device, device_id_type=MESH,
        )

    tile_row = lax.broadcasted_iota(jnp.int32, (8, 128), 0)
    lane = lax.broadcasted_iota(jnp.int32, (8, 128), 1)
    for number in range(5):
        for g in range(4):
            cells = [
                pd[4 * g + i] if number == 0 else pp[4 * g + i] if number == 4 else pv[4 * g + i, number - 1]
                for i in range(4)
            ]
            first, last = cells[0], cells[3]
            for i in (1, 2, 3):
                first = jnp.where(tile_row >= 2 * i, pltpu.roll(cells[i], 2 * i, 0), first)
            for i in (2, 1, 0):
                last = jnp.where(tile_row < 2 * i + 2, pltpu.roll(cells[i], 2 * i + 2, 0), last)
            spk[0, number, g] = first
            spk[1, number, g] = last
    pl.semaphore_wait(barrier, len(met))
    near = [
        send(spk.at[0], srv.at[1], 0, behind),
        send(spk.at[1], srv.at[0], 1, ahead),
        send(den.at[pl.ds(CELLS - 2, 2)], ld, 2, above),
        send(vel.at[pl.ds(CELLS - 2, 2)], lv, 3, above),
        send(pre.at[pl.ds(CELLS - 2, 2)], lp, 4, above),
        send(den.at[pl.ds(0, 2)], hd, 5, below),
        send(vel.at[pl.ds(0, 2)], hv, 6, below),
        send(pre.at[pl.ds(0, 2)], hp, 7, below),
    ]
    for copy in near:
        copy.start()
    loads[0].wait()

    def invert(g, carry):
        cells = pl.ds(4 * g, 4)
        inv = sym_inverse([kf[cells, i, j] for i in FIVE for j in range(i, 5)])
        inv = [v * (1.0 / DIFFUSION) for v in inv]
        for i in FIVE:
            for j in FIVE:
                comp[cells, i, j] = inv[tri(i, j)]
        return carry

    lax.fori_loop(0, CELLS // 4, invert, 0)

    zero = jnp.zeros((8, 128), jnp.float32)
    one = jnp.ones((8, 128), jnp.float32)
    unit = [jnp.stack([one if i == j else zero for j in FIVE]) for i in FIVE]
    empty = [jnp.stack([zero] * 5)] * 5

    def advance(j, state):
        u, q = state
        q = tuple(q[i] + u[i] for i in FIVE)
        u = tuple(u[i] + total(comp[j, i, k][None] * q[k] for k in FIVE) for i in FIVE)
        return u, q

    b_rows, d_rows = lax.fori_loop(0, CELLS, advance, (tuple(empty), tuple(unit)))
    b_inv = inverse([[b_rows[i][k] for k in FIVE] for i in FIVE])
    for i in FIVE:
        line = jnp.stack(b_inv[i])
        ee[core, LR + 5 * i : LR + 5 * i + 5] = -line
    b_inv_rows = [jnp.stack(b_inv[i]) for i in FIVE]
    for i in FIVE:
        t = RR + tri(i, i)
        ee[core, t : t + 5 - i] = total(d_rows[i][k][None] * b_inv_rows[k][i:] for k in FIVE)
        wp[5 * i : 5 * i + 5] = d_rows[i]
    a_rows, _ = lax.fori_loop(0, CELLS, advance, (tuple(unit), tuple(empty)))
    for i in FIVE:
        t = LL + tri(i, i)
        ee[core, t : t + 5 - i] = total(-ee[core, LR + 5 * i + k][None] * a_rows[k][i:] for k in FIVE)

    for copy in near:
        copy.wait()
    inner_low = jnp.where(me == 0, 0.0, 1.0).astype(jnp.float32)
    inner_high = jnp.where(me == count - 1, 0.0, 1.0).astype(jnp.float32)
    for c in range(2):
        fn[c] = jnp.stack(flux(ld[c], [lv[c, i] for i in range(3)], lp[c], 1)) * inner_low
        fn[CELLS + 2 + c] = jnp.stack(flux(hd[c], [hv[c, i] for i in range(3)], hp[c], 1)) * inner_high

    def normal_flux(j, carry):
        fn[j + 2] = jnp.stack(flux(pd[j], [pv[j, i] for i in range(3)], pp[j], 1))
        return carry

    lax.fori_loop(0, CELLS, normal_flux, 0, unroll=2)
    for side in range(2):
        edge = flux(srv[side, 0], [srv[side, 1 + i] for i in range(3)], srv[side, 4], 2)
        for number in range(5):
            gs[side, number] = edge[number]

    def residual(g, carry):
        low_edge = [gs[0, n, g] for n in FIVE]
        high_edge = [gs[1, n, g] for n in FIVE]
        for i in range(4):
            j = 4 * g + i
            v = [pv[j, a] for a in range(3)]
            along = flux(pd[j], v, pp[j], 0)
            across = flux(pd[j], v, pp[j], 2)
            for n in FIVE:
                f, h = along[n], across[n]
                s1 = jnp.where(lane < 127, pltpu.roll(f, 127, 1), 0.0) - jnp.where(lane > 0, pltpu.roll(f, 1, 1), 0.0)
                s2 = jnp.where(lane < 126, pltpu.roll(f, 126, 1), 0.0) - jnp.where(lane > 1, pltpu.roll(f, 2, 1), 0.0)
                up1 = jnp.where(tile_row < 7, pltpu.roll(h, 7, 0), pltpu.roll(high_edge[n], 7 - 2 * i, 0))
                up2 = jnp.where(tile_row < 6, pltpu.roll(h, 6, 0), pltpu.roll(high_edge[n], (14 - 2 * i) % 8, 0))
                dn1 = jnp.where(tile_row > 0, pltpu.roll(h, 1, 0), pltpu.roll(low_edge[n], 7 - 2 * i, 0))
                dn2 = jnp.where(tile_row > 1, pltpu.roll(h, 2, 0), pltpu.roll(low_edge[n], (8 - 2 * i) % 8, 0))
                t1 = s1 + (up1 - dn1) + (fn[j + 3, n] - fn[j + 1, n])
                t2 = s2 + (up2 - dn2) + (fn[j + 4, n] - fn[j, n])
                src[j, n] = t2 * (STEP / 12.0) - t1 * (8.0 * STEP / 12.0)
        return carry

    lax.fori_loop(0, CELLS // 4, residual, 0)

    def forced(j, state):
        u, q = state
        q = q + (u - src[j])
        u = u + total(comp[j, k] * q[k][None] for k in FIVE)
        return u, q

    a_load, b_load = lax.fori_loop(0, CELLS, forced, (empty[0], empty[0]))
    pull = [-total(ee[core, LR + 5 * i + k] * a_load[k] for k in FIVE) for i in FIVE]
    for i in FIVE:
        ee[core, RL + i] = -pull[i]
        ee[core, RH + i] = total(wp[5 * i + k] * pull[k] for k in FIVE) - b_load[i]

    swap = send(ee.at[core], ee.at[core], 8, partner)
    swap.start()
    swap.wait()

    def write(ref):
        def put(at, value):
            ref[at : at + value.shape[0]] = value

        return put

    def read(ref, *lead):
        return lambda at, size: ref[(*lead, slice(at, at + size))]

    combine(read(ee, 0), read(ee, 1), write(pe), write(wp))

    @pl.when(core == 0)
    def _():
        for s in range(ELEM):
            zs[pl.ds(s, 8, stride=ZROWS), :] = pe[s]
        copies = []
        for o in ORDER:
            there = lax.rem(z + o, NZ)
            copy = pltpu.make_async_remote_copy(
                src_ref=zs.at[pl.ds(pl.multiple_of(there * ZROWS, 8), ZROWS)],
                dst_ref=zr.at[pl.ds(pl.multiple_of(z * ZROWS, 8), ZROWS)],
                send_sem=z_send.at[o], recv_sem=z_recv.at[o],
                device_id=place(x, there, 0), device_id_type=MESH,
            )
            copy.start()
            copies.append(copy)
        mine = pl.ds(pl.multiple_of(z * ZROWS, 8), ZROWS)
        zr[mine] = zs[mine]
        for copy in copies:
            copy.wait()
        for s in range(ELEM):
            ze[s] = zr[pl.ds(s, 8, stride=ZROWS), :]

        def joined(ref, kept, levels):
            def level(step, carry):
                shift = 8 - lax.shift_left(1, step)

                def keep(at, value):
                    kept[step, at : at + value.shape[0]] = value

                combine(
                    read(ref),
                    lambda at, size: pltpu.roll(ref[at : at + size], shift, 1),
                    write(ref),
                    keep,
                )
                return carry

            lax.fori_loop(0, levels, level, 0)

        joined(ze, wz, 3)
        for s in range(ELEM):
            xs[s : s + 1, :] = ze[s, 0:1, :]
        copies = []
        for o in (2, 1, 3):
            copy = pltpu.make_async_remote_copy(
                src_ref=xs,
                dst_ref=xr.at[pl.ds(pl.multiple_of(x * ZROWS, 8), ZROWS)],
                send_sem=x_send.at[o], recv_sem=x_recv.at[o],
                device_id=place(lax.rem(x + o, NX), z, 0), device_id_type=MESH,
            )
            copy.start()
            copies.append(copy)
        xr[pl.ds(pl.multiple_of(x * ZROWS, 8), ZROWS)] = xs[...]
        for o in range(NX, 8):
            xr[pl.ds(o * ZROWS, ZROWS)] = xs[...]
        for copy in copies:
            copy.wait()
        for s in range(ELEM):
            xe[s] = xr[pl.ds(s, 8, stride=ZROWS), :]
        joined(xe, wx, 2)

        inv = sym_inverse([xe[LL + t] for t in range(15)])
        low = jnp.stack([total(inv[tri(i, k)] * xe[RL + k] for k in FIVE) for i in FIVE])
        high = jnp.zeros_like(low)

        def spread(kept, levels, low, high):
            def level(step, ends):
                low, high = ends
                at = levels - 1 - step
                gap = lax.shift_left(1, at)
                mid = middle_value(lambda a, size: kept[at, a : a + size], low, high)
                inside = (lax.bitwise_and(tile_row, gap) != 0)[None]
                return (
                    jnp.where(inside, pltpu.roll(mid, gap, 1), low),
                    jnp.where(inside, pltpu.roll(high, gap, 1), mid),
                )

            return lax.fori_loop(0, levels, level, (low, high))

        low, high = spread(wx, 2, low, high)
        low = pltpu.roll(low, 8 - x, 1)
        high = pltpu.roll(high, 8 - x, 1)
        low, high = spread(wz, 3, low, high)
        for i in FIVE:
            bs[pl.ds(i, 8, stride=BROWS), :] = low[i]
            bs[pl.ds(5 + i, 8, stride=BROWS), :] = high[i]
        mine = pl.ds(pl.multiple_of(z * BROWS, 8), BROWS)
        copies = []
        for o in ORDER + (0,):
            for c in range(NC):
                if o == 0 and c == 0:
                    continue
                there = lax.rem(z + o, NZ)
                copy = pltpu.make_async_remote_copy(
                    src_ref=bs.at[pl.ds(pl.multiple_of(there * BROWS, 8), BROWS)],
                    dst_ref=br.at[mine],
                    send_sem=b_send.at[o, c], recv_sem=b_recv.at[o],
                    device_id=place(x, there, c), device_id_type=MESH,
                )
                copy.start()
                copies.append(copy)
        br[mine] = bs[mine]
        for copy in copies:
            copy.wait_send()

    def arrival(o):
        there = lax.rem(z + o, NZ)
        return pltpu.make_async_remote_copy(
            src_ref=bs.at[pl.ds(0, BROWS)],
            dst_ref=br.at[pl.ds(pl.multiple_of(lax.rem(z + NZ - o, NZ) * BROWS, 8), BROWS)],
            send_sem=b_send.at[o, 0], recv_sem=b_recv.at[o],
            device_id=place(x, there, 1 - core), device_id_type=MESH,
        )

    for o in range(1, NZ):
        arrival(o).wait_recv()

    @pl.when(core == 1)
    def _():
        arrival(0).wait_recv()

    low = jnp.stack([br[pl.ds(i, 8, stride=BROWS), :] for i in FIVE])
    high = jnp.stack([br[pl.ds(5 + i, 8, stride=BROWS), :] for i in FIVE])
    mid = middle_value(read(wp), low, high)
    low, high = jnp.where(core == 0, low, mid), jnp.where(core == 0, mid, high)

    start = []
    for i in FIVE:
        own = total(ee[core, LL + tri(i, k)] * low[k] for k in FIVE)
        other = total(ee[core, LR + 5 * i + k] * high[k] for k in FIVE)
        start.append(ee[core, RL + i] - (own + other))

    def sweep(j, state):
        u, q = state
        out[j] = u
        q = q + (u - src[j])
        u = u + total(comp[j, k] * q[k][None] for k in FIVE)
        return u, q

    lax.fori_loop(0, CELLS, sweep, (low, jnp.stack(start)))


def shards(density, velocity, pressure, face_coef):
    f32 = jnp.float32
    shapes = [
        (CELLS, 5, 5, 8, 128), (CELLS, 8, 128), (CELLS, 3, 8, 128), (CELLS, 8, 128),
        (CELLS, 5, 5, 8, 128), (CELLS, 5, 8, 128), (CELLS + 4, 5, 8, 128),
        (2, 8, 128), (2, 3, 8, 128), (2, 8, 128), (2, 8, 128), (2, 3, 8, 128), (2, 8, 128),
        (2, 5, 4, 8, 128), (2, 5, 4, 8, 128), (2, 5, 4, 8, 128),
        (2, ELEM, 8, 128), (KEPT, 8, 128), (ELEM, 8, 128),
        (8 * ZROWS, 128), (8 * ZROWS, 128), (ELEM, 8, 128), (3, KEPT, 8, 128),
        (ZROWS, 128), (8 * ZROWS, 128), (ELEM, 8, 128), (2, KEPT, 8, 128),
        (8 * BROWS, 128), (8 * BROWS, 128),
    ]
    sems = [(4,), (9,), (9,), (8,), (8,), (4,), (4,), (8, 2), (8,)]
    return pl.pallas_call(
        kernel,
        out_shape=jax.ShapeDtypeStruct((CELLS, 5, 8, 128), f32),
        in_specs=[pl.BlockSpec(memory_space=pl.ANY)] * 4,
        out_specs=pl.BlockSpec(memory_space=pltpu.VMEM),
        scratch_shapes=[pltpu.VMEM(shape, f32) for shape in shapes]
        + [pltpu.SemaphoreType.DMA(shape) for shape in sems],
        compiler_params=pltpu.CompilerParams(collective_id=0, has_side_effects=True),
    )(density, velocity, pressure, face_coef)


def solution(mesh):
    return jax.shard_map(
        shards,
        mesh=mesh,
        in_specs=(
            P("normal", "span", None),
            P("normal", None, "span", None),
            P("normal", "span", None),
            P("normal", None, None, "span", None),
        ),
        out_specs=P("normal", None, "span", None),
        check_vma=False,
    )
```

```python
import jax
import jax.numpy as jnp
from jax import lax
from jax.experimental import pallas as pl
from jax.experimental.pallas import tpu as pltpu
from jax.sharding import PartitionSpec as P

MESH = pl.DeviceIdType.MESH
DIFFUSION = 1000.0
GAMMA = 1.4
STEP = 50.0
NX, NZ, NC, NS = 4, 8, 2, 4
CELLS = 16
FIVE = range(5)
LL, RR, LR, RL, RH, ELEM = 0, 15, 30, 55, 60, 65
MATS = 55
INV, MID, KEPT = 50, 65, 70
AROWS, BROWS = 56, 16
ORDER = (4, 3, 5, 2, 6, 1, 7)


def tri(i, j):
    low, high = min(i, j), max(i, j)
    return low * 5 - low * (low - 1) // 2 + high - low


def total(terms):
    terms = list(terms)
    while len(terms) > 1:
        terms = [a + b for a, b in zip(terms[::2], terms[1::2])] + terms[len(terms) & ~1 :]
    return terms[0]


def sym_inverse(upper):
    a = list(upper)
    for p in FIVE:
        d = 1.0 / a[tri(p, p)]
        row = [a[tri(p, j)] for j in FIVE]
        scaled = [row[j] * d for j in FIVE]
        for i in FIVE:
            for j in range(i, 5):
                if p not in (i, j):
                    a[tri(i, j)] = a[tri(i, j)] - scaled[i] * row[j]
        for j in FIVE:
            if j != p:
                a[tri(p, j)] = scaled[j]
        a[tri(p, p)] = -d
    return [-v for v in a]


def inverse(rows):
    a = [list(row) for row in rows]
    for p in FIVE:
        d = 1.0 / a[p][p]
        top = [d if j == p else a[p][j] * d for j in FIVE]
        for i in FIVE:
            if i != p:
                f = a[i][p]
                a[i] = [-f * d if j == p else a[i][j] - f * top[j] for j in FIVE]
        a[p] = top
    return a


def join_matrices(left, right, put, keep):
    middle = left(RR, 15) + right(LL, 15)
    inv = sym_inverse([middle[t] for t in range(15)])
    lr1 = [left(LR + 5 * i, 5) for i in FIVE]
    lr2 = [right(LR + 5 * i, 5) for i in FIVE]
    lt1 = [jnp.stack([lr1[i][k] for i in FIVE]) for k in FIVE]
    w1 = [total(inv[tri(i, k)][None] * lt1[k] for k in FIVE) for i in FIVE]
    w2 = [total(inv[tri(i, k)][None] * lr2[k] for k in FIVE) for i in FIVE]
    for t in range(15):
        keep(INV + t, inv[t][None])
    for i in FIVE:
        keep(5 * i, w1[i])
        keep(25 + 5 * i, w2[i])
    for i in FIVE:
        t = tri(i, i)
        put(LL + t, left(LL + t, 5 - i) - total(lr1[i][k][None] * w1[k][i:] for k in FIVE))
        put(RR + t, right(RR + t, 5 - i) - total(lr2[k][i][None] * w2[k][i:] for k in FIVE))
        put(LR + 5 * i, -total(lr1[i][k][None] * w2[k] for k in FIVE))


def join_loads(left, right, kept, put, keep):
    load = left(RH, 5) + right(RL, 5)
    low = left(RL, 5) - total(kept(5 * k, 5) * load[k][None] for k in FIVE)
    high = right(RH, 5) - total(kept(25 + 5 * k, 5) * load[k][None] for k in FIVE)
    for i in FIVE:
        keep(MID + i, total(kept(INV + tri(i, k), 1) * load[k][None] for k in FIVE))
    put(RL, low)
    put(RH, high)


def middle_value(kept, low, high):
    rows = []
    for i in FIVE:
        near, far = kept(5 * i, 5), kept(25 + 5 * i, 5)
        rows.append(kept(MID + i, 1)[0] - total(total((near * low, far * high))[k] for k in FIVE))
    return jnp.stack(rows)


def flux(d, v, p, direction):
    along = v[direction]
    energy = p / (GAMMA - 1.0) + 0.5 * d * (v[0] * v[0] + v[1] * v[1] + v[2] * v[2])
    carried = d * along
    pieces = [carried]
    for component in range(3):
        piece = carried * v[component]
        pieces.append(piece + p if component == direction else piece)
    pieces.append((energy + p) * along)
    return pieces


def kernel(
    den, vel, pre, fac, out,
    kf, pd, pv, pp, comp, src, fn, ld, lv, lp, hd, hv, hp, spk, srv, gs, ee, dm, wp, pe,
    za, zb, ra, rb, ze, wz, xa, xb, qa, qb, xe, wx, bs, br,
    load_sem, near_send, near_recv, z_send, z_recv, x_send, x_recv, b_send, b_recv, known,
):
    me, row = lax.axis_index("normal"), lax.axis_index("span")
    core = lax.rem(me, NC)
    z = lax.rem(lax.div(me, NC), NZ)
    x = lax.div(me, NC * NZ)
    count = NX * NZ * NC

    def place(x_at, z_at, core_at):
        return ((x_at * NZ + z_at) * NC + core_at, row)

    above = (lax.rem(me + 1, count), row)
    below = (lax.rem(me + count - 1, count), row)
    ahead = (me, lax.rem(row + 1, NS))
    behind = (me, lax.rem(row + NS - 1, NS))
    partner = place(x, z, 1 - core)

    beside = [place(x, lax.rem(z + o, NZ), core) for o in (1, NZ - 1)]
    across_x = [place(lax.rem(x + o, NX), z, core) for o in (1, NX - 1)]
    barrier = pltpu.get_barrier_semaphore()
    met = [above, below, ahead, behind, partner] + beside + across_x
    loads = [
        pltpu.make_async_copy(den, pd, load_sem.at[0]),
        pltpu.make_async_copy(vel, pv, load_sem.at[1]),
        pltpu.make_async_copy(pre, pp, load_sem.at[2]),
    ]
    blocks = [
        pltpu.make_async_copy(fac.at[pl.ds(4 * g, 4)], kf.at[pl.ds(4 * g, 4)], load_sem.at[3 + g])
        for g in range(CELLS // 4)
    ]
    for copy in loads + blocks:
        copy.start()
    for device in met:
        pl.semaphore_signal(barrier, inc=1, device_id=device, device_id_type=MESH)
    for copy in loads:
        copy.wait()

    def tell(stage, devices):
        for device in devices:
            pl.semaphore_signal(known.at[stage], inc=1, device_id=device, device_id_type=MESH)

    def hear(stage):
        pl.semaphore_wait(known.at[stage], 2)

    def send(source, target, number, device):
        return pltpu.make_async_remote_copy(
            src_ref=source, dst_ref=target, send_sem=near_send.at[number],
            recv_sem=near_recv.at[number], device_id=device, device_id_type=MESH,
        )

    tile_row = lax.broadcasted_iota(jnp.int32, (8, 128), 0)
    lane = lax.broadcasted_iota(jnp.int32, (8, 128), 1)
    for number in range(5):
        for g in range(4):
            cells = [
                pd[4 * g + i] if number == 0 else pp[4 * g + i] if number == 4 else pv[4 * g + i, number - 1]
                for i in range(4)
            ]
            first, last = cells[0], cells[3]
            for i in (1, 2, 3):
                first = jnp.where(tile_row >= 2 * i, pltpu.roll(cells[i], 2 * i, 0), first)
            for i in (2, 1, 0):
                last = jnp.where(tile_row < 2 * i + 2, pltpu.roll(cells[i], 2 * i + 2, 0), last)
            spk[0, number, g] = first
            spk[1, number, g] = last
    pl.semaphore_wait(barrier, len(met))
    near = [
        send(spk.at[0], srv.at[1], 0, behind),
        send(spk.at[1], srv.at[0], 1, ahead),
        send(den.at[pl.ds(CELLS - 2, 2)], ld, 2, above),
        send(vel.at[pl.ds(CELLS - 2, 2)], lv, 3, above),
        send(pre.at[pl.ds(CELLS - 2, 2)], lp, 4, above),
        send(den.at[pl.ds(0, 2)], hd, 5, below),
        send(vel.at[pl.ds(0, 2)], hv, 6, below),
        send(pre.at[pl.ds(0, 2)], hp, 7, below),
    ]
    for copy in near:
        copy.start()
    tell(0, beside)
    tell(3, across_x)

    def invert(g, carry):
        cells = pl.ds(4 * g, 4)
        pltpu.make_async_copy(fac.at[cells], kf.at[cells], load_sem.at[3 + g]).wait()
        inv = sym_inverse([kf[cells, i, j] for i in FIVE for j in range(i, 5)])
        inv = [v * (1.0 / DIFFUSION) for v in inv]
        for i in FIVE:
            for j in FIVE:
                comp[cells, i, j] = inv[tri(i, j)]
        return carry

    lax.fori_loop(0, CELLS // 4, invert, 0)
    hear(0)
    hear(3)
    tell(1, beside)

    zero = jnp.zeros((8, 128), jnp.float32)
    one = jnp.ones((8, 128), jnp.float32)
    unit = [jnp.stack([one if i == j else zero for j in FIVE]) for i in FIVE]
    empty = [jnp.stack([zero] * 5)] * 5

    def advance(j, state):
        u, q = state
        q = tuple(q[i] + u[i] for i in FIVE)
        u = tuple(u[i] + total(comp[j, i, k][None] * q[k] for k in FIVE) for i in FIVE)
        return u, q

    b_rows, d_rows = lax.fori_loop(0, CELLS, advance, (tuple(empty), tuple(unit)))
    b_inv = inverse([[b_rows[i][k] for k in FIVE] for i in FIVE])
    for i in FIVE:
        line = jnp.stack(b_inv[i])
        ee[core, LR + 5 * i : LR + 5 * i + 5] = -line
    b_inv_rows = [jnp.stack(b_inv[i]) for i in FIVE]
    for i in FIVE:
        t = RR + tri(i, i)
        ee[core, t : t + 5 - i] = total(d_rows[i][k][None] * b_inv_rows[k][i:] for k in FIVE)
        dm[5 * i : 5 * i + 5] = d_rows[i]
    hear(1)
    tell(2, beside)
    a_rows, _ = lax.fori_loop(0, CELLS, advance, (tuple(unit), tuple(empty)))
    for i in FIVE:
        t = LL + tri(i, i)
        ee[core, t : t + 5 - i] = total(-ee[core, LR + 5 * i + k][None] * a_rows[k][i:] for k in FIVE)

    swap = send(ee.at[core, pl.ds(0, MATS)], ee.at[core, pl.ds(0, MATS)], 8, partner)
    swap.start()

    def normal_flux(j, carry):
        fn[j + 2] = jnp.stack(flux(pd[j], [pv[j, i] for i in range(3)], pp[j], 1))
        return carry

    lax.fori_loop(0, CELLS, normal_flux, 0, unroll=2)

    for copy in near:
        copy.wait()
    inner_low = jnp.where(me == 0, 0.0, 1.0).astype(jnp.float32)
    inner_high = jnp.where(me == count - 1, 0.0, 1.0).astype(jnp.float32)
    for c in range(2):
        fn[c] = jnp.stack(flux(ld[c], [lv[c, i] for i in range(3)], lp[c], 1)) * inner_low
        fn[CELLS + 2 + c] = jnp.stack(flux(hd[c], [hv[c, i] for i in range(3)], hp[c], 1)) * inner_high
    for side in range(2):
        edge = flux(srv[side, 0], [srv[side, 1 + i] for i in range(3)], srv[side, 4], 2)
        for number in range(5):
            gs[side, number] = edge[number]

    def residual(g, carry):
        low_edge = [gs[0, n, g] for n in FIVE]
        high_edge = [gs[1, n, g] for n in FIVE]
        for i in range(4):
            j = 4 * g + i
            v = [pv[j, a] for a in range(3)]
            along = flux(pd[j], v, pp[j], 0)
            across = flux(pd[j], v, pp[j], 2)
            for n in FIVE:
                f, h = along[n], across[n]
                s1 = jnp.where(lane < 127, pltpu.roll(f, 127, 1), 0.0) - jnp.where(lane > 0, pltpu.roll(f, 1, 1), 0.0)
                s2 = jnp.where(lane < 126, pltpu.roll(f, 126, 1), 0.0) - jnp.where(lane > 1, pltpu.roll(f, 2, 1), 0.0)
                up1 = jnp.where(tile_row < 7, pltpu.roll(h, 7, 0), pltpu.roll(high_edge[n], 7 - 2 * i, 0))
                up2 = jnp.where(tile_row < 6, pltpu.roll(h, 6, 0), pltpu.roll(high_edge[n], (14 - 2 * i) % 8, 0))
                dn1 = jnp.where(tile_row > 0, pltpu.roll(h, 1, 0), pltpu.roll(low_edge[n], 7 - 2 * i, 0))
                dn2 = jnp.where(tile_row > 1, pltpu.roll(h, 2, 0), pltpu.roll(low_edge[n], (8 - 2 * i) % 8, 0))
                t1 = s1 + (up1 - dn1) + (fn[j + 3, n] - fn[j + 1, n])
                t2 = s2 + (up2 - dn2) + (fn[j + 4, n] - fn[j, n])
                src[j, n] = t2 * (STEP / 12.0) - t1 * (8.0 * STEP / 12.0)
        return carry

    lax.fori_loop(0, CELLS // 4, residual, 0)

    def forced(j, state):
        u, q = state
        q = q + (u - src[j])
        u = u + total(comp[j, k] * q[k][None] for k in FIVE)
        return u, q

    a_load, b_load = lax.fori_loop(0, CELLS, forced, (empty[0], empty[0]))
    pull = [-total(ee[core, LR + 5 * i + k] * a_load[k] for k in FIVE) for i in FIVE]
    for i in FIVE:
        ee[core, RL + i] = -pull[i]
        ee[core, RH + i] = total(dm[5 * i + k] * pull[k] for k in FIVE) - b_load[i]

    swap_loads = send(ee.at[core, pl.ds(MATS, 10)], ee.at[core, pl.ds(MATS, 10)], 9, partner)
    swap_loads.start()

    def write(ref, *lead):
        def put(at, value):
            ref[(*lead, slice(at, at + value.shape[0]))] = value

        return put

    def read(ref, *lead):
        return lambda at, size: ref[(*lead, slice(at, at + size))]

    swap.wait()
    join_matrices(read(ee, 0), read(ee, 1), write(pe), write(wp))
    hear(2)

    def part(at, rows):
        return pl.ds(pl.multiple_of(at * rows, 8), rows)

    def to_owners(kind, source, target, rows):
        copies = []
        for o in ORDER:
            there = lax.rem(z + o, NZ)
            copy = pltpu.make_async_remote_copy(
                src_ref=source.at[part(there, rows)], dst_ref=target.at[part(z, rows)],
                send_sem=z_send.at[kind, o], recv_sem=z_recv.at[kind, o],
                device_id=place(x, there, 0), device_id_type=MESH,
            )
            copy.start()
            copies.append(copy)
        target[part(z, rows)] = source[part(z, rows)]
        return copies

    def to_columns(kind, source, target, rows):
        copies = []
        for o in (2, 1, 3):
            copy = pltpu.make_async_remote_copy(
                src_ref=source, dst_ref=target.at[part(x, rows)],
                send_sem=x_send.at[kind, o], recv_sem=x_recv.at[kind, o],
                device_id=place(lax.rem(x + o, NX), z, 0), device_id_type=MESH,
            )
            copy.start()
            copies.append(copy)
        target[part(x, rows)] = source[...]
        for o in range(NX, 8):
            target[pl.ds(o * rows, rows)] = source[...]
        return copies

    def turned(ref, step):
        shift = 8 - lax.shift_left(1, step)
        return lambda at, size: pltpu.roll(ref[at : at + size], shift, 1)

    def matrix_levels(ref, kept, levels):
        def level(step, carry):
            join_matrices(read(ref), turned(ref, step), write(ref), write(kept, step))
            return carry

        lax.fori_loop(0, levels, level, 0)

    def load_levels(ref, kept, levels):
        def level(step, carry):
            join_loads(read(ref), turned(ref, step), read(kept, step), write(ref), write(kept, step))
            return carry

        lax.fori_loop(0, levels, level, 0)

    @pl.when(core == 0)
    def _():
        for s in range(MATS):
            za[pl.ds(s, 8, stride=AROWS), :] = pe[s]
        to_owner = to_owners(0, za, ra, AROWS)
        swap_loads.wait()
        join_loads(read(ee, 0), read(ee, 1), read(wp), write(pe), write(wp))
        for s in range(10):
            zb[pl.ds(s, 8, stride=BROWS), :] = pe[MATS + s]
        loads_to_owner = to_owners(1, zb, rb, BROWS)
        for copy in to_owner:
            copy.wait()
        for s in range(MATS):
            ze[s] = ra[pl.ds(s, 8, stride=AROWS), :]
        matrix_levels(ze, wz, 3)
        for s in range(MATS):
            xa[s : s + 1, :] = ze[s, 0:1, :]
        to_column = to_columns(0, xa, qa, AROWS)
        for copy in loads_to_owner:
            copy.wait()
        for s in range(10):
            ze[MATS + s] = rb[pl.ds(s, 8, stride=BROWS), :]
        load_levels(ze, wz, 3)
        for s in range(10):
            xb[s : s + 1, :] = ze[MATS + s, 0:1, :]
        loads_to_column = to_columns(1, xb, qb, BROWS)
        for copy in to_column:
            copy.wait()
        for s in range(MATS):
            xe[s] = qa[pl.ds(s, 8, stride=AROWS), :]
        matrix_levels(xe, wx, 2)
        inv = sym_inverse([xe[LL + t] for t in range(15)])
        for copy in loads_to_column:
            copy.wait()
        for s in range(10):
            xe[MATS + s] = qb[pl.ds(s, 8, stride=BROWS), :]
        load_levels(xe, wx, 2)

        low = jnp.stack([total(inv[tri(i, k)] * xe[RL + k] for k in FIVE) for i in FIVE])
        high = jnp.zeros_like(low)

        def spread(kept, levels, low, high):
            def level(step, ends):
                low, high = ends
                at = levels - 1 - step
                gap = lax.shift_left(1, at)
                mid = middle_value(lambda a, size: kept[at, a : a + size], low, high)
                inside = (lax.bitwise_and(tile_row, gap) != 0)[None]
                return (
                    jnp.where(inside, pltpu.roll(mid, gap, 1), low),
                    jnp.where(inside, pltpu.roll(high, gap, 1), mid),
                )

            return lax.fori_loop(0, levels, level, (low, high))

        low, high = spread(wx, 2, low, high)
        low = pltpu.roll(low, 8 - x, 1)
        high = pltpu.roll(high, 8 - x, 1)
        low, high = spread(wz, 3, low, high)
        for i in FIVE:
            bs[pl.ds(i, 8, stride=BROWS), :] = low[i]
            bs[pl.ds(5 + i, 8, stride=BROWS), :] = high[i]
        def serve(there):
            for c in range(NC):
                pltpu.make_async_remote_copy(
                    src_ref=bs.at[pl.ds(there * BROWS, BROWS)], dst_ref=br.at[part(z, BROWS)],
                    send_sem=b_send.at[there, c], recv_sem=b_recv.at[z],
                    device_id=place(x, there, c), device_id_type=MESH,
                ).start()

        for there in (0, 1, 2, 3, 7, 4, 6, 5):
            pl.when(there != z)(lambda there=there: serve(there))
        at_home = pltpu.make_async_remote_copy(
            src_ref=bs.at[part(z, BROWS)], dst_ref=br.at[part(z, BROWS)],
            send_sem=b_send.at[z, 1], recv_sem=b_recv.at[z],
            device_id=partner, device_id_type=MESH,
        )
        at_home.start()
        br[part(z, BROWS)] = bs[part(z, BROWS)]

    @pl.when(core == 1)
    def _():
        swap_loads.wait()
        join_loads(read(ee, 0), read(ee, 1), read(wp), write(pe), write(wp))

    def arrival(k):
        return pltpu.make_async_remote_copy(
            src_ref=bs.at[pl.ds(k * BROWS, BROWS)], dst_ref=br.at[pl.ds(k * BROWS, BROWS)],
            send_sem=b_send.at[k, 0], recv_sem=b_recv.at[k],
            device_id=partner, device_id_type=MESH,
        )

    for k in range(NZ):
        pl.when(jnp.logical_or(k != z, core == 1))(lambda k=k: arrival(k).wait_recv())

    low = jnp.stack([br[pl.ds(i, 8, stride=BROWS), :] for i in FIVE])
    high = jnp.stack([br[pl.ds(5 + i, 8, stride=BROWS), :] for i in FIVE])
    mid = middle_value(read(wp), low, high)
    low, high = jnp.where(core == 0, low, mid), jnp.where(core == 0, mid, high)

    start = []
    for i in FIVE:
        own = total(ee[core, LL + tri(i, k)] * low[k] for k in FIVE)
        other = total(ee[core, LR + 5 * i + k] * high[k] for k in FIVE)
        start.append(ee[core, RL + i] - (own + other))

    def sweep(j, state):
        u, q = state
        out[j] = u
        q = q + (u - src[j])
        u = u + total(comp[j, k] * q[k][None] for k in FIVE)
        return u, q

    lax.fori_loop(0, CELLS, sweep, (low, jnp.stack(start)))

    @pl.when(core == 0)
    def _():
        def sent(there, c):
            return pltpu.make_async_remote_copy(
                src_ref=bs.at[pl.ds(there * BROWS, BROWS)], dst_ref=br.at[pl.ds(there * BROWS, BROWS)],
                send_sem=b_send.at[there, c], recv_sem=b_recv.at[there],
                device_id=partner, device_id_type=MESH,
            )

        for there in range(NZ):
            pl.when(there != z)(lambda there=there: sent(there, 0).wait_send())
            sent(there, 1).wait_send()


def shards(density, velocity, pressure, face_coef):
    f32 = jnp.float32
    shapes = [
        (CELLS, 5, 5, 8, 128), (CELLS, 8, 128), (CELLS, 3, 8, 128), (CELLS, 8, 128),
        (CELLS, 5, 5, 8, 128), (CELLS, 5, 8, 128), (CELLS + 4, 5, 8, 128),
        (2, 8, 128), (2, 3, 8, 128), (2, 8, 128), (2, 8, 128), (2, 3, 8, 128), (2, 8, 128),
        (2, 5, 4, 8, 128), (2, 5, 4, 8, 128), (2, 5, 4, 8, 128),
        (2, ELEM, 8, 128), (25, 8, 128), (KEPT, 8, 128), (ELEM, 8, 128),
        (8 * AROWS, 128), (8 * BROWS, 128), (8 * AROWS, 128), (8 * BROWS, 128),
        (ELEM, 8, 128), (3, KEPT, 8, 128),
        (AROWS, 128), (BROWS, 128), (8 * AROWS, 128), (8 * BROWS, 128), (ELEM, 8, 128), (2, KEPT, 8, 128),
        (8 * BROWS, 128), (8 * BROWS, 128),
    ]
    sems = [(7,), (10,), (10,), (2, 8), (2, 8), (2, 4), (2, 4), (8, 2), (8,)]
    return pl.pallas_call(
        kernel,
        out_shape=pltpu.VMEM((CELLS, 5, 8, 128), f32),
        in_specs=[pl.BlockSpec(memory_space=pl.ANY)] * 4,
        out_specs=pl.BlockSpec(memory_space=pltpu.VMEM),
        scratch_shapes=[pltpu.VMEM(shape, f32) for shape in shapes]
        + [pltpu.SemaphoreType.DMA(shape) for shape in sems]
        + [pltpu.SemaphoreType.REGULAR((4,))],
        compiler_params=pltpu.CompilerParams(collective_id=0, has_side_effects=True),
    )(density, velocity, pressure, face_coef)


def solution(mesh):
    return jax.shard_map(
        shards,
        mesh=mesh,
        in_specs=(
            P("normal", "span", None),
            P("normal", None, "span", None),
            P("normal", "span", None),
            P("normal", None, None, "span", None),
        ),
        out_specs=P("normal", None, "span", None),
        check_vma=False,
    )
```

```python
import jax
import jax.numpy as jnp
from jax import lax
from jax.experimental import pallas as pl
from jax.experimental.pallas import tpu as pltpu
from jax.sharding import PartitionSpec as P

MESH = pl.DeviceIdType.MESH
DIFFUSION = 1000.0
GAMMA = 1.4
STEP = 50.0
NX, NZ, NC, NS = 4, 8, 2, 4
CELLS = 16
FAR, NEAR = STEP / 12.0, 8.0 * STEP / 12.0
FIVE = range(5)
LL, RR, LR, RL, RH, ELEM = 0, 15, 30, 55, 60, 65
MATS = 55
INV, MID, KEPT = 50, 65, 70
AROWS, BROWS = 56, 16
ORDER = (4, 3, 5, 2, 6, 1, 7)


def tri(i, j):
    low, high = min(i, j), max(i, j)
    return low * 5 - low * (low - 1) // 2 + high - low


def total(terms):
    terms = list(terms)
    while len(terms) > 1:
        terms = [a + b for a, b in zip(terms[::2], terms[1::2])] + terms[len(terms) & ~1 :]
    return terms[0]


def sym_inverse(upper):
    a = list(upper)
    for p in FIVE:
        d = 1.0 / a[tri(p, p)]
        row = [a[tri(p, j)] for j in FIVE]
        scaled = [row[j] * d for j in FIVE]
        for i in FIVE:
            for j in range(i, 5):
                if p not in (i, j):
                    a[tri(i, j)] = a[tri(i, j)] - scaled[i] * row[j]
        for j in FIVE:
            if j != p:
                a[tri(p, j)] = scaled[j]
        a[tri(p, p)] = -d
    return [-v for v in a]


def inverse(rows):
    a = [list(row) for row in rows]
    for p in FIVE:
        d = 1.0 / a[p][p]
        top = [d if j == p else a[p][j] * d for j in FIVE]
        for i in FIVE:
            if i != p:
                f = a[i][p]
                a[i] = [-f * d if j == p else a[i][j] - f * top[j] for j in FIVE]
        a[p] = top
    return a


def join_matrices(left, right, put, keep):
    middle = left(RR, 15) + right(LL, 15)
    inv = sym_inverse([middle[t] for t in range(15)])
    lr1 = [left(LR + 5 * i, 5) for i in FIVE]
    lr2 = [right(LR + 5 * i, 5) for i in FIVE]
    lt1 = [jnp.stack([lr1[i][k] for i in FIVE]) for k in FIVE]
    w1 = [total(inv[tri(i, k)][None] * lt1[k] for k in FIVE) for i in FIVE]
    w2 = [total(inv[tri(i, k)][None] * lr2[k] for k in FIVE) for i in FIVE]
    for t in range(15):
        keep(INV + t, inv[t][None])
    for i in FIVE:
        keep(5 * i, w1[i])
        keep(25 + 5 * i, w2[i])
    for i in FIVE:
        t = tri(i, i)
        put(LL + t, left(LL + t, 5 - i) - total(lr1[i][k][None] * w1[k][i:] for k in FIVE))
        put(RR + t, right(RR + t, 5 - i) - total(lr2[k][i][None] * w2[k][i:] for k in FIVE))
        put(LR + 5 * i, -total(lr1[i][k][None] * w2[k] for k in FIVE))


def join_loads(left, right, kept, put, keep):
    load = left(RH, 5) + right(RL, 5)
    low = left(RL, 5) - total(kept(5 * k, 5) * load[k][None] for k in FIVE)
    high = right(RH, 5) - total(kept(25 + 5 * k, 5) * load[k][None] for k in FIVE)
    for i in FIVE:
        keep(MID + i, total(kept(INV + tri(i, k), 1) * load[k][None] for k in FIVE))
    put(RL, low)
    put(RH, high)


def middle_value(kept, low, high):
    rows = []
    for i in FIVE:
        near, far = kept(5 * i, 5), kept(25 + 5 * i, 5)
        rows.append(kept(MID + i, 1)[0] - total(total((near * low, far * high))[k] for k in FIVE))
    return jnp.stack(rows)


def flux(d, v, p, direction):
    along = v[direction]
    energy = p / (GAMMA - 1.0) + 0.5 * d * (v[0] * v[0] + v[1] * v[1] + v[2] * v[2])
    carried = d * along
    pieces = [carried]
    for component in range(3):
        piece = carried * v[component]
        pieces.append(piece + p if component == direction else piece)
    pieces.append((energy + p) * along)
    return pieces


def kernel(
    den, vel, pre, fac, out,
    kf, pd, pv, pp, comp, src, fn, ld, lv, lp, hd, hv, hp, spk, srv, gs, ee, dm, wp, pe,
    za, zb, ra, rb, ze, wz, xa, xb, qa, qb, xe, wx, bs, br,
    load_sem, near_send, near_recv, z_send, z_recv, x_send, x_recv, b_send, b_recv, known,
):
    me, row = lax.axis_index("normal"), lax.axis_index("span")
    core = lax.rem(me, NC)
    z = lax.rem(lax.div(me, NC), NZ)
    x = lax.div(me, NC * NZ)
    count = NX * NZ * NC

    def place(x_at, z_at, core_at):
        return ((x_at * NZ + z_at) * NC + core_at, row)

    above = (lax.rem(me + 1, count), row)
    below = (lax.rem(me + count - 1, count), row)
    ahead = (me, lax.rem(row + 1, NS))
    behind = (me, lax.rem(row + NS - 1, NS))
    partner = place(x, z, 1 - core)

    beside = [place(x, lax.rem(z + o, NZ), core) for o in (1, NZ - 1)]
    two_off = [place(x, lax.rem(z + o, NZ), core) for o in (2, NZ - 2)]
    across_x = [place(lax.rem(x + o, NX), z, core) for o in (1, NX - 1)]
    barrier = pltpu.get_barrier_semaphore()
    met = [above, below, ahead, behind, partner] + beside + across_x
    loads = [
        pltpu.make_async_copy(den, pd, load_sem.at[0]),
        pltpu.make_async_copy(vel, pv, load_sem.at[1]),
        pltpu.make_async_copy(pre, pp, load_sem.at[2]),
    ]
    blocks = [
        pltpu.make_async_copy(fac.at[pl.ds(4 * g, 4)], kf.at[pl.ds(4 * g, 4)], load_sem.at[3 + g])
        for g in range(CELLS // 4)
    ]
    for copy in loads + blocks:
        copy.start()
    for device in met:
        pl.semaphore_signal(barrier, inc=1, device_id=device, device_id_type=MESH)
    def tell(stage, devices):
        for device in devices:
            pl.semaphore_signal(known.at[stage], inc=1, device_id=device, device_id_type=MESH)

    def hear(stage):
        pl.semaphore_wait(known.at[stage], 2)

    def send(source, target, number, device):
        return pltpu.make_async_remote_copy(
            src_ref=source, dst_ref=target, send_sem=near_send.at[number],
            recv_sem=near_recv.at[number], device_id=device, device_id_type=MESH,
        )

    pl.semaphore_wait(barrier, len(met))
    tell(0, beside)
    tell(2, across_x)
    near = [
        send(spk.at[0], srv.at[1], 0, behind),
        send(spk.at[1], srv.at[0], 1, ahead),
        send(den.at[pl.ds(CELLS - 2, 2)], ld, 2, above),
        send(vel.at[pl.ds(CELLS - 2, 2)], lv, 3, above),
        send(pre.at[pl.ds(CELLS - 2, 2)], lp, 4, above),
        send(den.at[pl.ds(0, 2)], hd, 5, below),
        send(vel.at[pl.ds(0, 2)], hv, 6, below),
        send(pre.at[pl.ds(0, 2)], hp, 7, below),
    ]
    for copy in near[2:]:
        copy.start()
    for copy in loads:
        copy.wait()

    tile_row = lax.broadcasted_iota(jnp.int32, (8, 128), 0)
    lane = lax.broadcasted_iota(jnp.int32, (8, 128), 1)
    for number in range(5):
        for g in range(4):
            cells = [
                pd[4 * g + i] if number == 0 else pp[4 * g + i] if number == 4 else pv[4 * g + i, number - 1]
                for i in range(4)
            ]
            first, last = cells[0], cells[3]
            for i in (1, 2, 3):
                first = jnp.where(tile_row >= 2 * i, pltpu.roll(cells[i], 2 * i, 0), first)
            for i in (2, 1, 0):
                last = jnp.where(tile_row < 2 * i + 2, pltpu.roll(cells[i], 2 * i + 2, 0), last)
            spk[0, number, g] = first
            spk[1, number, g] = last
    for copy in near[:2]:
        copy.start()

    def invert(g, carry):
        cells = pl.ds(4 * g, 4)
        pltpu.make_async_copy(fac.at[cells], kf.at[cells], load_sem.at[3 + g]).wait()
        inv = sym_inverse([kf[cells, i, j] for i in FIVE for j in range(i, 5)])
        inv = [v * (1.0 / DIFFUSION) for v in inv]
        for i in FIVE:
            for j in FIVE:
                comp[cells, i, j] = inv[tri(i, j)]
        return carry

    lax.fori_loop(0, CELLS // 4, invert, 0)
    hear(0)
    tell(1, two_off)

    zero = jnp.zeros((8, 128), jnp.float32)
    one = jnp.ones((8, 128), jnp.float32)
    unit = [jnp.stack([one if i == j else zero for j in FIVE]) for i in FIVE]
    empty = [jnp.stack([zero] * 5)] * 5

    def advance(j, state):
        u, q = state
        q = tuple(q[i] + u[i] for i in FIVE)
        u = tuple(u[i] + total(comp[j, i, k][None] * q[k] for k in FIVE) for i in FIVE)
        return u, q

    b_rows, d_rows = lax.fori_loop(0, CELLS, advance, (tuple(empty), tuple(unit)))
    b_inv = inverse([[b_rows[i][k] for k in FIVE] for i in FIVE])
    for i in FIVE:
        line = jnp.stack(b_inv[i])
        ee[core, LR + 5 * i : LR + 5 * i + 5] = -line
    b_inv_rows = [jnp.stack(b_inv[i]) for i in FIVE]
    for i in FIVE:
        t = RR + tri(i, i)
        ee[core, t : t + 5 - i] = total(d_rows[i][k][None] * b_inv_rows[k][i:] for k in FIVE)
        dm[5 * i : 5 * i + 5] = d_rows[i]
    swaps = [
        send(ee.at[core, pl.ds(RR, 40)], ee.at[core, pl.ds(RR, 40)], 8, partner),
        send(ee.at[core, pl.ds(LL, 15)], ee.at[core, pl.ds(LL, 15)], 9, partner),
        send(ee.at[core, pl.ds(MATS, 10)], ee.at[core, pl.ds(MATS, 10)], 10, partner),
    ]
    swaps[0].start()
    a_rows, _ = lax.fori_loop(0, CELLS, advance, (tuple(unit), tuple(empty)))
    for i in FIVE:
        t = LL + tri(i, i)
        ee[core, t : t + 5 - i] = total(-ee[core, LR + 5 * i + k][None] * a_rows[k][i:] for k in FIVE)

    swaps[1].start()

    def normal_flux(j, carry):
        fn[j + 2] = jnp.stack(flux(pd[j], [pv[j, i] for i in range(3)], pp[j], 1))
        return carry

    lax.fori_loop(0, CELLS, normal_flux, 0, unroll=2)

    nothing = jnp.zeros((5, 8, 128), jnp.float32)
    for j in (0, 1, CELLS + 2, CELLS + 3):
        fn[j] = nothing

    def residual(g, carry):
        for i in range(4):
            j = 4 * g + i
            v = [pv[j, a] for a in range(3)]
            along = flux(pd[j], v, pp[j], 0)
            across = flux(pd[j], v, pp[j], 2)
            for n in FIVE:
                f, h = along[n], across[n]
                s1 = jnp.where(lane < 127, pltpu.roll(f, 127, 1), 0.0) - jnp.where(lane > 0, pltpu.roll(f, 1, 1), 0.0)
                s2 = jnp.where(lane < 126, pltpu.roll(f, 126, 1), 0.0) - jnp.where(lane > 1, pltpu.roll(f, 2, 1), 0.0)
                up1 = jnp.where(tile_row < 7, pltpu.roll(h, 7, 0), 0.0)
                up2 = jnp.where(tile_row < 6, pltpu.roll(h, 6, 0), 0.0)
                dn1 = jnp.where(tile_row > 0, pltpu.roll(h, 1, 0), 0.0)
                dn2 = jnp.where(tile_row > 1, pltpu.roll(h, 2, 0), 0.0)
                t1 = s1 + (up1 - dn1) + (fn[j + 3, n] - fn[j + 1, n])
                t2 = s2 + (up2 - dn2) + (fn[j + 4, n] - fn[j, n])
                src[j, n] = t2 * FAR - t1 * NEAR
        return carry

    lax.fori_loop(0, CELLS // 4, residual, 0)

    for copy in near:
        copy.wait()
    inner_low = jnp.where(me == 0, 0.0, 1.0).astype(jnp.float32)
    inner_high = jnp.where(me == count - 1, 0.0, 1.0).astype(jnp.float32)
    below_flux, above_flux = [], []
    for c in range(2):
        below_flux.append(jnp.stack(flux(ld[c], [lv[c, i] for i in range(3)], lp[c], 1)) * inner_low)
        above_flux.append(jnp.stack(flux(hd[c], [hv[c, i] for i in range(3)], hp[c], 1)) * inner_high)
    src[0] = src[0] + (below_flux[1] * NEAR - below_flux[0] * FAR)
    src[1] = src[1] - below_flux[1] * FAR
    src[CELLS - 2] = src[CELLS - 2] + above_flux[0] * FAR
    src[CELLS - 1] = src[CELLS - 1] + (above_flux[1] * FAR - above_flux[0] * NEAR)
    odd = lax.rem(tile_row, 2) == 1
    for side in range(2):
        edge = flux(srv[side, 0], [srv[side, 1 + i] for i in range(3)], srv[side, 4], 2)
        for n in FIVE:
            for g in range(4):
                value = edge[n][g]
                if side == 0:
                    gs[side, n, g] = jnp.where(odd, 0.0, pltpu.roll(value, 7, 0) * NEAR) - value * FAR
                else:
                    gs[side, n, g] = value * FAR - jnp.where(odd, pltpu.roll(value, 1, 0) * NEAR, 0.0)

    def span_edges(g, carry):
        for n in FIVE:
            low, high = gs[0, n, g], gs[1, n, g]
            for i in range(4):
                first = low if i == 0 else pltpu.roll(low, 8 - 2 * i, 0)
                last = high if i == 3 else pltpu.roll(high, 6 - 2 * i, 0)
                reach = jnp.where(tile_row < 2, first, jnp.where(tile_row > 5, last, 0.0))
                src[4 * g + i, n] = src[4 * g + i, n] + reach
        return carry

    lax.fori_loop(0, CELLS // 4, span_edges, 0)

    def forced(j, state):
        u, q = state
        q = q + (u - src[j])
        u = u + total(comp[j, k] * q[k][None] for k in FIVE)
        return u, q

    a_load, b_load = lax.fori_loop(0, CELLS, forced, (empty[0], empty[0]), unroll=4)
    pull = [-total(ee[core, LR + 5 * i + k] * a_load[k] for k in FIVE) for i in FIVE]
    for i in FIVE:
        ee[core, RL + i] = -pull[i]
        ee[core, RH + i] = total(dm[5 * i + k] * pull[k] for k in FIVE) - b_load[i]

    swaps[2].start()

    def write(ref, *lead):
        def put(at, value):
            ref[(*lead, slice(at, at + value.shape[0]))] = value

        return put

    def read(ref, *lead):
        return lambda at, size: ref[(*lead, slice(at, at + size))]

    swaps[0].wait()
    swaps[1].wait()
    join_matrices(read(ee, 0), read(ee, 1), write(pe), write(wp))
    hear(1)
    hear(2)

    def part(at, rows):
        return pl.ds(pl.multiple_of(at * rows, 8), rows)

    owner = core == lax.rem(z, 2)

    def to_owner(kind, source, target, rows, o):
        there = lax.rem(z + o, NZ)
        return pltpu.make_async_remote_copy(
            src_ref=source.at[part(there, rows)], dst_ref=target.at[part(z, rows)],
            send_sem=z_send.at[kind, o], recv_sem=z_recv.at[kind, o],
            device_id=place(x, there, core), device_id_type=MESH,
        )

    def to_owners(*piece):
        @pl.when(owner)
        def _():
            kind, source, target, rows = piece
            for o in (4, 6, 2):
                to_owner(*piece, o).start()
            target[part(z, rows)] = source[part(z, rows)]

        @pl.when(jnp.logical_not(owner))
        def _():
            for o in (3, 5, 1, 7):
                to_owner(*piece, o).start()

    def at_owner(*piece):
        for o in (1, 7, 2, 6, 3, 5, 4):
            to_owner(*piece, o).wait_recv()

    def sent_to_owners(*piece):
        @pl.when(owner)
        def _():
            for o in (4, 6, 2):
                to_owner(*piece, o).wait_send()

        @pl.when(jnp.logical_not(owner))
        def _():
            for o in (3, 5, 1, 7):
                to_owner(*piece, o).wait_send()

    def to_columns(kind, source, target, rows):
        copies = []
        for o in (2, 1, 3):
            copy = pltpu.make_async_remote_copy(
                src_ref=source, dst_ref=target.at[part(x, rows)],
                send_sem=x_send.at[kind, o], recv_sem=x_recv.at[kind, o],
                device_id=place(lax.rem(x + o, NX), z, core), device_id_type=MESH,
            )
            copy.start()
            copies.append(copy)
        target[part(x, rows)] = source[...]
        for o in range(NX, 8):
            target[pl.ds(o * rows, rows)] = source[...]
        return copies

    def turned(ref, step):
        shift = 8 - (1 << step)
        return lambda at, size: pltpu.roll(ref[at : at + size], shift, 1)

    def matrix_levels(ref, kept, levels):
        def level(step, carry):
            join_matrices(read(ref), turned(ref, step), write(ref), write(kept, step))
            return carry

        for step in range(levels):
            level(step, 0)

    def load_levels(ref, kept, levels):
        def level(step, carry):
            join_loads(read(ref), turned(ref, step), read(kept, step), write(ref), write(kept, step))
            return carry

        for step in range(levels):
            level(step, 0)

    pieces = [(0, za, ra, AROWS), (1, zb, rb, BROWS)]
    for s in range(MATS):
        za[pl.ds(s, 8, stride=AROWS), :] = pe[s]
    to_owners(*pieces[0])
    swaps[2].wait()
    join_loads(read(ee, 0), read(ee, 1), read(wp), write(pe), write(wp))
    for s in range(10):
        zb[pl.ds(s, 8, stride=BROWS), :] = pe[MATS + s]
    to_owners(*pieces[1])

    @pl.when(owner)
    def _():
        at_owner(*pieces[0])
        for s in range(MATS):
            ze[s] = ra[pl.ds(s, 8, stride=AROWS), :]
        matrix_levels(ze, wz, 3)
        for s in range(MATS):
            xa[s : s + 1, :] = ze[s, 0:1, :]
        to_column = to_columns(0, xa, qa, AROWS)
        at_owner(*pieces[1])
        for s in range(10):
            ze[MATS + s] = rb[pl.ds(s, 8, stride=BROWS), :]
        load_levels(ze, wz, 3)
        for s in range(10):
            xb[s : s + 1, :] = ze[MATS + s, 0:1, :]
        loads_to_column = to_columns(1, xb, qb, BROWS)
        for copy in to_column:
            copy.wait()
        for s in range(MATS):
            xe[s] = qa[pl.ds(s, 8, stride=AROWS), :]
        matrix_levels(xe, wx, 2)
        inv = sym_inverse([xe[LL + t] for t in range(15)])
        for copy in loads_to_column:
            copy.wait()
        for s in range(10):
            xe[MATS + s] = qb[pl.ds(s, 8, stride=BROWS), :]
        load_levels(xe, wx, 2)

        low = jnp.stack([total(inv[tri(i, k)] * xe[RL + k] for k in FIVE) for i in FIVE])
        high = jnp.zeros_like(low)

        def spread(kept, levels, low, high):
            def level(step, ends):
                low, high = ends
                at = levels - 1 - step
                gap = 1 << at
                mid = middle_value(lambda a, size: kept[at, a : a + size], low, high)
                inside = (lax.bitwise_and(tile_row, gap) != 0)[None]
                return (
                    jnp.where(inside, pltpu.roll(mid, gap, 1), low),
                    jnp.where(inside, pltpu.roll(high, gap, 1), mid),
                )

            for step in range(levels):
                low, high = level(step, (low, high))
            return low, high

        low, high = spread(wx, 2, low, high)
        low = pltpu.roll(low, 8 - x, 1)
        high = pltpu.roll(high, 8 - x, 1)
        low, high = spread(wz, 3, low, high)
        for i in FIVE:
            bs[pl.ds(i, 8, stride=BROWS), :] = low[i]
            bs[pl.ds(5 + i, 8, stride=BROWS), :] = high[i]
        at_home = pltpu.make_async_remote_copy(
            src_ref=bs.at[part(z, BROWS)], dst_ref=br.at[part(z, BROWS)],
            send_sem=b_send.at[z, 0], recv_sem=b_recv.at[z],
            device_id=partner, device_id_type=MESH,
        )
        at_home.start()
        def serve(there):
            for c in (1, 0):
                pltpu.make_async_remote_copy(
                    src_ref=bs.at[pl.ds(there * BROWS, BROWS)], dst_ref=br.at[part(z, BROWS)],
                    send_sem=b_send.at[there, c], recv_sem=b_recv.at[z],
                    device_id=place(x, there, c), device_id_type=MESH,
                ).start()

        for there in (0, 1, 2, 3, 7, 4, 6, 5):
            pl.when(there != z)(lambda there=there: serve(there))
        br[part(z, BROWS)] = bs[part(z, BROWS)]

    def arrival(k):
        return pltpu.make_async_remote_copy(
            src_ref=bs.at[pl.ds(k * BROWS, BROWS)], dst_ref=br.at[pl.ds(k * BROWS, BROWS)],
            send_sem=b_send.at[k, 0], recv_sem=b_recv.at[k],
            device_id=partner, device_id_type=MESH,
        )

    for k in range(NZ):
        pl.when(jnp.logical_or(k != z, jnp.logical_not(owner)))(lambda k=k: arrival(k).wait_recv())

    low = jnp.stack([br[pl.ds(i, 8, stride=BROWS), :] for i in FIVE])
    high = jnp.stack([br[pl.ds(5 + i, 8, stride=BROWS), :] for i in FIVE])
    mid = middle_value(read(wp), low, high)
    low, high = jnp.where(core == 0, low, mid), jnp.where(core == 0, mid, high)

    start = []
    for i in FIVE:
        own = total(ee[core, LL + tri(i, k)] * low[k] for k in FIVE)
        other = total(ee[core, LR + 5 * i + k] * high[k] for k in FIVE)
        start.append(ee[core, RL + i] - (own + other))

    def sweep(j, state):
        u, q = state
        out[j] = u
        q = q + (u - src[j])
        u = u + total(comp[j, k] * q[k][None] for k in FIVE)
        return u, q

    lax.fori_loop(0, CELLS, sweep, (low, jnp.stack(start)), unroll=4)

    for piece in pieces:
        sent_to_owners(*piece)

    @pl.when(owner)
    def _():
        def sent(there, c):
            return pltpu.make_async_remote_copy(
                src_ref=bs.at[pl.ds(there * BROWS, BROWS)], dst_ref=br.at[pl.ds(there * BROWS, BROWS)],
                send_sem=b_send.at[there, c], recv_sem=b_recv.at[there],
                device_id=partner, device_id_type=MESH,
            )

        for there in range(NZ):
            sent(there, 0).wait_send()
            pl.when(there != z)(lambda there=there: sent(there, 1).wait_send())


def shards(density, velocity, pressure, face_coef):
    f32 = jnp.float32
    shapes = [
        (CELLS, 5, 5, 8, 128), (CELLS, 8, 128), (CELLS, 3, 8, 128), (CELLS, 8, 128),
        (CELLS, 5, 5, 8, 128), (CELLS, 5, 8, 128), (CELLS + 4, 5, 8, 128),
        (2, 8, 128), (2, 3, 8, 128), (2, 8, 128), (2, 8, 128), (2, 3, 8, 128), (2, 8, 128),
        (2, 5, 4, 8, 128), (2, 5, 4, 8, 128), (2, 5, 4, 8, 128),
        (2, ELEM, 8, 128), (25, 8, 128), (KEPT, 8, 128), (ELEM, 8, 128),
        (8 * AROWS, 128), (8 * BROWS, 128), (8 * AROWS, 128), (8 * BROWS, 128),
        (ELEM, 8, 128), (3, KEPT, 8, 128),
        (AROWS, 128), (BROWS, 128), (8 * AROWS, 128), (8 * BROWS, 128), (ELEM, 8, 128), (2, KEPT, 8, 128),
        (8 * BROWS, 128), (8 * BROWS, 128),
    ]
    sems = [(7,), (11,), (11,), (2, 8), (2, 8), (2, 4), (2, 4), (8, 2), (8,)]
    return pl.pallas_call(
        kernel,
        out_shape=pltpu.VMEM((CELLS, 5, 8, 128), f32),
        in_specs=[pl.BlockSpec(memory_space=pl.ANY)] * 4,
        out_specs=pl.BlockSpec(memory_space=pltpu.VMEM),
        scratch_shapes=[pltpu.VMEM(shape, f32) for shape in shapes]
        + [pltpu.SemaphoreType.DMA(shape) for shape in sems]
        + [pltpu.SemaphoreType.REGULAR((4,))],
        compiler_params=pltpu.CompilerParams(collective_id=0, has_side_effects=True),
    )(density, velocity, pressure, face_coef)


def solution(mesh):
    return jax.shard_map(
        shards,
        mesh=mesh,
        in_specs=(
            P("normal", "span", None),
            P("normal", None, "span", None),
            P("normal", "span", None),
            P("normal", None, None, "span", None),
        ),
        out_specs=P("normal", None, "span", None),
        check_vma=False,
    )
```
